128 devices in a mesh: seq: 32 (over z, x, core), dp: 4 (over y).
Axes of the slice: x: 4, y: 4, z: 4, core: 2. Of those that a mesh axis runs over, the one named last changes fastest.
Arguments:
- queries: bfloat16 [4, 8192, 1536], P('dp', 'seq'), may hold values from -6 to 6
- key_vectors: bfloat16 [4, 8192, 1536], P('dp', 'seq'), may hold values from -6 to 6
- value_vectors: bfloat16 [4, 8192, 1536], P('dp', 'seq'), may hold values from -6 to 6
- features: bfloat16 [4, 8192, 2048], P('dp', 'seq'), may hold values from -6 to 6
- w_level: bfloat16 [2048, 144], replicated, may hold values from -0.125 to 0.125
- offsets: int32 [4, 64], P('dp', 'seq'), may hold values from 0 to 128, as said below
- cotangent: bfloat16 [4, 8192, 1536], P('dp', 'seq'), may hold values from -6 to 6
- final_grad: bfloat16 [4, 12, 128, 128], P('dp'), may hold values from -6 to 6
Outputs:
- normed: bfloat16 [4, 8192, 1536], P('dp', 'seq')
- grad_query: bfloat16 [4, 8192, 1536], P('dp', 'seq')
- grad_key: bfloat16 [4, 8192, 1536], P('dp', 'seq')
- grad_value: bfloat16 [4, 8192, 1536], P('dp', 'seq')
- grad_level: float32 [2048, 144], P('seq')
- final_state: float32 [4, 12, 128, 128], P('dp')
The draws below stay inside these ranges and needn't reach their ends.
Inputs may be any that keep to these rules, and one draw needn't show every extreme that they name: `offsets`: each stretch of 128 positions holds at most one document start, at the given place; the value 128 means that none starts in the stretch.
All inputs are finite; a program needn't handle non-finite values.
Results may differ from the reference program's by a relative error of at most 0.001.
Values sent between devices are 32-bit elements; how exact they have to be, the bound alone decides.
No kernel may reach another device: no remote copies, remote signals or barrier semaphores. Data moves between devices by JAX's collectives and lax.ppermute only.
A program may use at most 128 MiB of HBM per device.

```python
import jax
import jax.numpy as jnp
from jax import lax

D = 2048
HEADS = 12
HEAD_DIM = 128
STRETCH = 128
LEVELS = 12
BATCH = 4
NCH = 64
SEQLEN = 8192


def draw_offsets(key, part):
    first_key, second_key = jax.random.split(jax.random.fold_in(key, 17))
    places = jax.random.randint(first_key, (BATCH, NCH), 0, STRETCH, dtype=jnp.int32)
    picked = jax.random.randint(second_key, (BATCH, NCH), 0, 10, dtype=jnp.int32) == 0
    return jnp.where(picked, places, STRETCH).astype(jnp.int32)


def with_spikes(values, stream_key, source, target, shards_of, factor):
    def block_of(dim):
        return (jnp.arange(values.shape[dim]) // (values.shape[dim] // shards_of)).reshape((-1,) + (1,) * (values.ndim - 1 - dim))

    one_side = jax.random.permutation(stream_key, shards_of)[block_of(target)]
    far = (block_of(target) + shards_of // 2) % shards_of
    return jnp.where((block_of(source) == one_side) | (block_of(source) == far), factor * values, values)


def steps_of(key, dims, shards, least, high):
    def one(dim, shards_of):
        draws = jax.random.uniform(jax.random.fold_in(jax.random.fold_in(key, 6), dim), (shards_of,), jnp.float32, least / len(shards), high / len(shards))
        return jnp.repeat(jnp.exp(draws), dims[dim] // shards_of).reshape((-1,) + (1,) * (len(dims) - dim - 1))

    factor_of = one(*shards[0])
    for cut in shards[1:]:
        factor_of = factor_of * one(*cut)
    return factor_of


def scatter_about(stream_key, shape, scale, reach, cuts=(), kind=jnp.bfloat16):
    result = scale * jax.random.normal(stream_key, shape, jnp.float32)
    if cuts:
        result = result * steps_of(stream_key, shape, cuts, -0.22, 0.18)
    return jnp.clip(result, -reach, reach).astype(kind)


def noise_with(rng, shape, spread, most, pieces, heavy, kind=jnp.bfloat16):
    drawn = spread * jax.random.normal(rng, shape, jnp.float32)
    if pieces:
        drawn = drawn * steps_of(rng, shape, pieces, -0.22, 0.18)
    return jnp.clip(with_spikes(drawn, jax.random.fold_in(rng, 3), *heavy), -most, most).astype(kind)


def setup_inputs(seed: int = 0) -> dict:
    key_list = jax.random.split(jax.random.key(seed), 9)
    return {
        "queries": scatter_about(key_list[0], (BATCH, SEQLEN, HEADS * HEAD_DIM), 1.0, 6.0, ((0, 4), (1, 32))),
        "key_vectors": scatter_about(key_list[1], (BATCH, SEQLEN, HEADS * HEAD_DIM), 1.0, 6.0, ((0, 4), (1, 32))),
        "value_vectors": scatter_about(key_list[2], (BATCH, SEQLEN, HEADS * HEAD_DIM), 1.0, 6.0, ((0, 4), (1, 32))),
        "features": noise_with(key_list[3], (BATCH, SEQLEN, D), 1.0, 6.0, ((0, 4), (1, 32)), (1, 2, 32, 2.75)),
        "w_level": scatter_about(key_list[4], (D, LEVELS * HEADS), D ** -0.5, 0.125),
        "offsets": draw_offsets(jax.random.fold_in(key_list[8], 71), 0),
        "cotangent": scatter_about(key_list[6], (BATCH, SEQLEN, HEADS * HEAD_DIM), 1.0, 6.0, ((0, 4), (1, 32))),
        "final_grad": scatter_about(key_list[7], (BATCH, HEADS, HEAD_DIM, HEAD_DIM), 1.0, 6.0, ((0, 4),)),
    }


highest = lax.Precision.HIGHEST
epsilon = 1e-06
state_scale = 0.0625

def normalize(summed):
    return summed * lax.rsqrt(lax.optimization_barrier(jnp.mean(summed * summed, -1, keepdims=True)) + epsilon)

def sequence_forward(query_f, key_f, value_f, level_gate, offsets):
    shaped = (NCH, STRETCH, HEADS, HEAD_DIM)
    query_c = query_f.reshape(shaped)
    key_c = key_f.reshape(shaped)
    value_c = value_f.reshape(shaped)
    gates = level_gate.reshape(NCH, STRETCH, LEVELS, HEADS)
    position = jnp.arange(STRETCH, dtype=jnp.int32)
    has_reset = offsets < STRETCH
    after_start = position[None, :] >= offsets[:, None]
    key_kept = jnp.logical_or(jnp.logical_not(has_reset)[:, None], after_start).astype(jnp.float32)
    query_open = jnp.logical_not(jnp.logical_and(has_reset[:, None], after_start)).astype(jnp.float32)
    tails = jnp.einsum('cshp,cshr->chpr', key_c * key_kept[:, :, None, None], value_c, precision=highest)
    scores = jnp.einsum('cthp,cshp->chts', query_c, key_c, precision=highest)
    causal = position[:, None] >= position[None, :]
    cut_off = has_reset[:, None, None] & after_start[:, :, None] & jnp.logical_not(after_start)[:, None, :]
    allowed = jnp.logical_and(causal[None], jnp.logical_not(cut_off)).astype(jnp.float32)
    intra_gate = jnp.transpose(gates[:, :, 0, :], (0, 2, 1))
    weights = scores * allowed[:, None] * intra_gate[:, :, :, None]
    summed = jnp.einsum('chts,cshr->cthr', weights, value_c, precision=highest)
    stretch_index = jnp.arange(NCH, dtype=jnp.int32)
    marks = jnp.where(has_reset, stretch_index, -1).astype(jnp.int32)
    before = jnp.concatenate([jnp.full((1,), -1, jnp.int32), lax.cummax(marks)[:-1]])
    blocks = tails
    flags = has_reset
    for bit_index in range(NCH.bit_length() - 1):
        owner = jnp.right_shift(stretch_index, bit_index)
        chosen = jnp.maximum(owner - 1, 0).astype(jnp.int32)
        usable = jnp.logical_and(owner % 2 == 1, before < jnp.left_shift(owner, bit_index)).astype(jnp.float32)
        state = blocks[chosen]
        product = jnp.einsum('cthp,chpr->cthr', query_c, state, precision=highest)
        scaled = gates[:, :, bit_index + 1, :] * query_open[:, :, None] * usable[:, None, None]
        summed = summed + scaled[..., None] * product
        lower = blocks[0::2]
        upper = blocks[1::2]
        blocks = jnp.where(flags[1::2][:, None, None, None], upper, lower + upper)
        flags = jnp.logical_or(flags[0::2], flags[1::2])
    return (summed.reshape(SEQLEN, HEADS * HEAD_DIM), blocks[0] * state_scale)

def one_sequence(inputs, w_full):
    queries, key_vectors, value_vectors, features, offsets, cotangent, final_grad = inputs
    feat_f = features.astype(jnp.float32)

    def forward(query_f, key_f, value_f, w_f):
        level_gate = jax.nn.softplus(jnp.dot(feat_f, w_f, precision=highest))
        mixed, final_state = sequence_forward(query_f, key_f, value_f, level_gate, offsets)
        normed = normalize(mixed.reshape(SEQLEN, HEADS, HEAD_DIM)).reshape(SEQLEN, HEADS * HEAD_DIM)
        return (normed, final_state)
    outputs, pullback = jax.vjp(forward, queries.astype(jnp.float32), key_vectors.astype(jnp.float32), value_vectors.astype(jnp.float32), w_full)
    grads = pullback((cotangent.astype(jnp.float32), final_grad.astype(jnp.float32)))
    return (outputs[0].astype(jnp.bfloat16), grads[0].astype(jnp.bfloat16), grads[1].astype(jnp.bfloat16), grads[2].astype(jnp.bfloat16), grads[3], outputs[1])

def reference(queries, key_vectors, value_vectors, features, w_level, offsets, cotangent, final_grad):
    w_full = w_level.astype(jnp.float32)
    results = lax.map(lambda inputs: one_sequence(inputs, w_full), (queries, key_vectors, value_vectors, features, offsets, cotangent, final_grad))
    return (results[0], results[1], results[2], results[3], lax.optimization_barrier(jnp.sum(results[4], 0)), results[5])
```

```python
import jax
import jax.numpy as jnp
from jax import lax
from jax.experimental import pallas as pl
from jax.experimental.pallas import tpu as pltpu
from jax.sharding import PartitionSpec as P

HEADS = 12
HALF = HEADS // 2
HD = 128
STRETCH = 128
ROWS = 2 * STRETCH
LEVELS = 12
BITS = 5
HROWS = HALF * HD
FROWS = HEADS * HD
SHARE = 64
EPS = 1e-06
SCALE = 0.0625
F32 = jnp.float32
BF16 = jnp.bfloat16

NN = (((1,), (0,)), ((), ()))
NT = (((1,), (1,)), ((), ()))
TN = (((0,), (0,)), ((), ()))


def dot(a, b, dims=NN):
    return lax.dot_general(a, b, dims, preferred_element_type=F32)


def split(a):
    high = a.astype(BF16)
    return high, (a - high.astype(F32)).astype(BF16)


def split3(a):
    high = a.astype(BF16)
    rest = a - high.astype(F32)
    middle = rest.astype(BF16)
    return high, middle, (rest - middle.astype(F32)).astype(BF16)


def lanes(*parts):
    return jnp.concatenate(parts, axis=1)


def rows(*parts):
    return jnp.concatenate(parts, axis=0)


def seq_index():
    return lax.axis_index("seq").astype(jnp.int32)


def bit_of(b):
    return lax.rem(lax.shift_right_logical(seq_index(), b), 2)


def core():
    return bit_of(0)


def chip_x():
    return lax.rem(lax.shift_right_logical(seq_index(), 1), 4)


def chip_z():
    return lax.shift_right_logical(seq_index(), 3)


def sds(shape, dtype=F32):
    return jax.ShapeDtypeStruct(shape, dtype)


def call(kernel, out_shape, *args, scratch=(), flops=0, name=None, smem=()):
    outs = out_shape if isinstance(out_shape, (list, tuple)) else [out_shape]
    size = sum(a.size * a.dtype.itemsize for a in args)
    size += sum(s.size * jnp.dtype(s.dtype).itemsize for s in outs)
    in_specs = [
        pl.BlockSpec(memory_space=pltpu.SMEM if n in smem else pltpu.VMEM) for n in range(len(args))
    ]
    out_specs = [pl.BlockSpec(memory_space=pltpu.VMEM) for _ in outs]
    with jax.named_scope(name):
        return pl.pallas_call(
            kernel,
            in_specs=in_specs,
            out_specs=out_specs if isinstance(out_shape, (list, tuple)) else out_specs[0],
            scratch_shapes=list(scratch),
            out_shape=out_shape,
            compiler_params=pltpu.CompilerParams(vmem_limit_bytes=16 * 2**20),
            cost_estimate=pl.CostEstimate(flops=flops, bytes_accessed=size, transcendentals=0),
            name=name,
        )(*args)


def per_head(step, unroll=2):
    half = core() * HALF

    def own_half(n, carry):
        step(n, half + n, True)
        return carry

    def other_half(n, carry):
        step(n, HALF - half + n, False)
        return carry

    lax.fori_loop(0, HALF, own_half, 0, unroll=unroll)
    lax.fori_loop(0, HALF, other_half, 0, unroll=unroll)


def cut(n):
    return pl.ds(pl.multiple_of(n * HD, HD), HD)


def tails_kernel(off_ref, k_ref, v_ref, o_ref, keys_ref, open_ref, pair_ref):
    off0, off1 = off_ref[0, 0], off_ref[0, 1]
    t = lax.broadcasted_iota(jnp.int32, (ROWS, HD), 0)
    second = t >= STRETCH
    u = jnp.where(second, t - STRETCH, t)
    off = jnp.where(second, off1, off0)
    inside = jnp.where(off < STRETCH, jnp.where(u >= off, 1.0, 0.0), 0.0)
    kept = jnp.where(off < STRETCH, inside, 1.0)
    f0, f1 = (off0 < STRETCH).astype(F32), (off1 < STRETCH).astype(F32)
    keys = kept * jnp.where(second, 1.0, 1.0 - f1)
    keys_ref[...] = keys
    open_ref[...] = (1.0 - inside) * jnp.where(second, 1.0 - f0, 1.0)

    def head(h, carry):
        kept_keys = (k_ref[:, cut(h)].astype(F32) * keys).astype(BF16)
        o_ref[cut(h), :] = dot(kept_keys, v_ref[:, cut(h)], TN)
        return carry

    lax.fori_loop(0, HEADS, head, 0, unroll=3)
    o_ref[FROWS : FROWS + 8, :] = jnp.full((8, HD), jnp.maximum(f0, f1), F32)

    t = lax.broadcasted_iota(jnp.int32, (ROWS, ROWS), 0)
    s = lax.broadcasted_iota(jnp.int32, (ROWS, ROWS), 1)
    t2, s2 = t >= STRETCH, s >= STRETCH
    ut, us = jnp.where(t2, t - STRETCH, t), jnp.where(s2, s - STRETCH, s)
    t_off, s_off = jnp.where(t2, off1, off0), jnp.where(s2, off1, off0)
    t_in = jnp.where(t_off < STRETCH, jnp.where(ut >= t_off, 1, 0), 0)
    s_in = jnp.where(s_off < STRETCH, jnp.where(us >= s_off, 1, 0), 0)
    s_kept = jnp.where(s_off < STRETCH, s_in, 1)
    same = jnp.where(ut >= us, 1, 0) * (1 - t_in * (1 - s_in))
    cross = (1 - t_in) * s_kept * jnp.where(t2, 1, 0)
    both = jnp.where(t2, 1, 0) == jnp.where(s2, 1, 0)
    pair_ref[...] = jnp.where(both, same, cross).astype(F32)


def tails(offsets, k, v):
    return call(
        tails_kernel,
        [sds((FROWS + 8, HD)), sds((ROWS, HD)), sds((ROWS, HD)), sds((ROWS, ROWS))],
        offsets, k, v, flops=2 * ROWS * HD * FROWS, name="tails", smem=(0,),
    )


def joined(own, other, own_flag, other_flag, upper):
    own_by = jnp.where(upper, jnp.ones_like(other_flag), 1.0 - other_flag)
    other_by = jnp.where(upper, 1.0 - own_flag, jnp.ones_like(own_flag))
    return own * own_by + other * other_by


def join_first_kernel(a_ref, b_ref, o_ref):
    upper = core() == 1
    half = pl.ds(pl.multiple_of(core() * HROWS, HROWS), HROWS)
    af, bf = a_ref[FROWS:, :], b_ref[FROWS:, :]
    o_ref[:HROWS, :] = joined(a_ref[half, :], b_ref[half, :], af[0:1], bf[0:1], upper)
    o_ref[HROWS:, :] = jnp.maximum(af, bf)


def join_kernel(bit):
    def kernel(a_ref, b_ref, o_ref):
        upper = bit_of(bit) == 1
        af, bf = a_ref[HROWS:, :], b_ref[HROWS:, :]
        o_ref[:HROWS, :] = joined(a_ref[:HROWS, :], b_ref[:HROWS, :], af[0:1], bf[0:1], upper)
        o_ref[HROWS:, :] = jnp.maximum(af, bf)

    return kernel


def join(own, other, bit):
    kernel = join_kernel(bit) if bit else join_first_kernel
    return call(kernel, sds((HROWS + 8, HD)), own, other, flops=4 * HROWS * HD, name=f"join{bit}")


def gates_kernel(x_ref, w_ref, gate_ref, slope_ref):
    logit = dot(x_ref[...], w_ref[:HD, :], NT)
    gate_ref[...] = jax.nn.softplus(logit)
    slope_ref[...] = 1.0 / (1.0 + jnp.exp(-logit))


def gates(x, w):
    return call(
        gates_kernel, [sds((ROWS, HD))] * 2, x, w, flops=2 * x.size * HD, name="gates"
    )


def head_columns(gate_ref, h):
    return pltpu.roll(gate_ref[...], lax.rem(HD - h, HD), axis=1)


def column(rolled, slot):
    return rolled[:, slot * HEADS : slot * HEADS + 1]


def local_weights(q, k, gate_cols, mask):
    first = lax.broadcasted_iota(jnp.int32, (ROWS, 1), 0) < STRETCH
    g0, g1 = column(gate_cols, 0), column(gate_cols, 1)
    left = jnp.where(first, g0, g1)
    raw = dot(q, k, NT) * mask
    return raw, left, g0, first


def by_columns(a, left, right):
    return lanes(a[:, :HD] * left, a[:, HD:] * right)


def intra_kernel(q_ref, k_ref, v_ref, pair_ref, same_ref, near_ref):
    low, high = slice(0, STRETCH), slice(STRETCH, ROWS)

    def head(h, carry):
        raw = dot(q_ref[:, cut(h)], k_ref[:, cut(h)], NT) * pair_ref[...]
        v0, v1 = v_ref[low, cut(h)], v_ref[high, cut(h)]
        for out, a, v in (
            (same_ref.at[low, cut(h)], raw[low, :HD], v0),
            (same_ref.at[high, cut(h)], raw[high, HD:], v1),
            (near_ref.at[:, cut(h)], raw[high, :HD], v0),
        ):
            out[...] = dot(lanes(*split3(a)), rows(v, v, v))
        return carry

    lax.fori_loop(0, HEADS, head, 0, unroll=2)


def intra(q, k, v, pair):
    return call(
        intra_kernel, [sds((ROWS, FROWS)), sds((STRETCH, FROWS))], q, k, v, pair,
        flops=6 * ROWS * ROWS * FROWS, name="intra",
    )


def usable_rows(flags):
    prefix = jnp.zeros((1, HD), F32)
    result = []
    for b, flag in enumerate(flags):
        upper = bit_of(b).astype(F32)
        result.append(upper * (1.0 - prefix))
        prefix = jnp.maximum(prefix, upper * flag)
    return result


def flag_rows(first_ref, own_refs):
    return [first_ref[FROWS : FROWS + 1, :]] + [r[HROWS : HROWS + 1, :] for r in own_refs]


def level_weight(cols, mask, usable, b):
    return column(cols, 2 + b) * (mask * usable)


def state_products(q, states):
    high, middle, low = zip(*[split3(s) for s in states])
    return dot(lanes(q, q, q), rows(lanes(*high), lanes(*middle), lanes(*low)))


def low_levels_kernel(
    same_ref, near_ref, q_ref, gate_ref, open_ref, s0, a1, a2, a3, o1, o2, o3, mix_ref, p0, p1, p2, p3
):
    usable = usable_rows(flag_rows(s0, (a1, a2, a3)))
    mask = open_ref[...]

    def step(n, h, own):
        cols = head_columns(gate_ref, h)
        refs = (a1, a2, a3) if own else (o1, o2, o3)
        states = [s0[cut(h), :]] + [r[cut(n), :] for r in refs]
        prod = state_products(q_ref[:, cut(h)], states)
        near = column(cols, 1)[STRETCH:] * near_ref[:, cut(h)]
        mixed = column(cols, 0) * same_ref[:, cut(h)] + rows(jnp.zeros((STRETCH, HD), F32), near)
        for b, ref in enumerate((p0, p1, p2, p3)):
            part = prod[:, b * HD : (b + 1) * HD]
            ref[:, cut(h)] = part
            mixed = mixed + level_weight(cols, mask, usable[b], b) * part
        mix_ref[:, cut(h)] = mixed

    per_head(step)


def low_levels(same, near, q, gate, is_open, first, own, other):
    return call(
        low_levels_kernel, [sds((ROWS, FROWS))] * 5, same, near, q, gate, is_open, first, *own,
        *other, flops=16 * ROWS * HD * FROWS, name="low_levels",
    )


def top_level_kernel(
    mix_ref, q_ref, g_ref, gate_ref, open_ref, s0, a1, a2, a3, a4, o4, norm_ref, dsum_ref, p4,
    da4, do4
):
    usable = usable_rows(flag_rows(s0, (a1, a2, a3, a4)))
    mask = open_ref[...]

    def step(n, h, own):
        cols = head_columns(gate_ref, h)
        weight = level_weight(cols, mask, usable[4], 4)
        q = q_ref[:, cut(h)]
        prod = state_products(q, [(a4 if own else o4)[cut(n), :]])
        p4[:, cut(h)] = prod
        mixed = mix_ref[:, cut(h)] + weight * prod
        scale = lax.rsqrt(jnp.mean(mixed * mixed, axis=1, keepdims=True) + EPS)
        normed = mixed * scale
        norm_ref[:, cut(h)] = normed.astype(BF16)
        g = g_ref[:, cut(h)].astype(F32)
        dsum = scale * (g - normed * jnp.mean(g * normed, axis=1, keepdims=True))
        dsum_ref[:, cut(h)] = dsum
        high, low = split(weight * dsum)
        (da4 if own else do4)[cut(n), :] = dot(rows(q, q), rows(high, low), TN)

    per_head(step)


def top_level(mix, q, g, gate, is_open, first, own, other4):
    wide = sds((ROWS, FROWS))
    return call(
        top_level_kernel,
        [sds((ROWS, FROWS), BF16), wide, wide, sds((HROWS, HD)), sds((HROWS, HD))],
        mix, q, g, gate, is_open, first, *own, other4, flops=8 * ROWS * HD * FROWS,
        name="top_level",
    )


def gate_grads_kernel(
    dsum_ref, same_ref, near_ref, p0, p1, p2, p3, p4, slope_ref, open_ref, s0, a1, a2, a3, a4, out
):
    usable = usable_rows(flag_rows(s0, (a1, a2, a3, a4)))
    lane = lax.broadcasted_iota(jnp.int32, (ROWS, HD), 1)
    out[...] = jnp.zeros((ROWS, HD), F32)

    def head(h, carry):
        dsum = dsum_ref[:, cut(h)]
        near = jnp.sum(dsum[STRETCH:] * near_ref[:, cut(h)], axis=1, keepdims=True)
        values = [
            jnp.sum(dsum * same_ref[:, cut(h)], axis=1, keepdims=True),
            rows(jnp.zeros((STRETCH, 1), F32), near),
        ]
        for ref in (p0, p1, p2, p3, p4):
            values.append(jnp.sum(dsum * ref[:, cut(h)], axis=1, keepdims=True))
        spread = out[...]
        for slot, value in enumerate(values):
            spread = jnp.where(lane == slot * HEADS + h, value, spread)
        out[...] = spread
        return carry

    lax.fori_loop(0, HEADS, head, 0, unroll=2)
    factor = slope_ref[...]
    mask = open_ref[...]
    for b in range(BITS):
        start = (2 + b) * HEADS
        at_level = jnp.where(lane >= start, jnp.where(lane < start + HEADS, 1.0, 0.0), 0.0)
        factor = factor * (1.0 - at_level + at_level * (mask * usable[b]))
    out[...] = out[...] * factor


def gate_grads(dsum, same, near, prods, slope, is_open, first, own):
    return call(
        gate_grads_kernel, sds((ROWS, HD)), dsum, same, near, *prods, slope, is_open, first, *own,
        flops=14 * ROWS * FROWS, name="gate_grads",
    )


def state_grads_kernel(
    q_ref, dsum_ref, gate_ref, open_ref, s0, a1, a2, a3, d0, da1, da2, da3, do1, do2, do3
):
    usable = usable_rows(flag_rows(s0, (a1, a2, a3)))
    mask = open_ref[...]

    def step(n, h, own):
        cols = head_columns(gate_ref, h)
        dsum = dsum_ref[:, cut(h)]
        parts = [level_weight(cols, mask, usable[b], b) * dsum for b in range(4)]
        high, low = split(lanes(*parts))
        q = q_ref[:, cut(h)]
        grad = dot(rows(q, q), rows(high, low), TN)
        d0[cut(h), :] = grad[:, :HD]
        for m, ref in enumerate((da1, da2, da3) if own else (do1, do2, do3)):
            ref[cut(n), :] = grad[:, (m + 1) * HD : (m + 2) * HD]

    per_head(step)


def state_grads(q, dsum, gate, is_open, first, own):
    half = sds((HROWS, HD))
    return call(
        state_grads_kernel, [sds((FROWS, HD))] + [half] * 6, q, dsum, gate, is_open, first, *own,
        flops=16 * ROWS * HD * FROWS, name="state_grads",
    )


def back_kernel(bit):
    def kernel(*refs):
        if bit == BITS - 1:
            fg_ref, own_ref, got_ref, b_ref, p_ref, to_ref, keep_ref = refs
            on_first = (lax.shift_right_logical(seq_index(), 1) == 0).astype(F32)
            half = pl.ds(pl.multiple_of(core() * HROWS, HROWS), HROWS)
            w = fg_ref[half, :].astype(F32) * (SCALE * on_first)
        else:
            w1_ref, w2_ref, own_ref, got_ref, b_ref, p_ref, to_ref, keep_ref = refs
            w = w1_ref[...] + w2_ref[...]
        upper = bit_of(bit) == 1
        own_keep = 1.0 - b_ref[HROWS : HROWS + 1, :]
        partner_keep = 1.0 - p_ref[HROWS : HROWS + 1, :]
        one = jnp.ones_like(own_keep)
        grad = (own_ref[...] + got_ref[...]) * upper.astype(F32)
        to_ref[...] = w * jnp.where(upper, own_keep, one) + grad
        keep_ref[...] = w * jnp.where(upper, one, partner_keep)

    return kernel


def back(bit, ws, own, got, block, partner):
    return call(
        back_kernel(bit), [sds((HROWS, HD))] * 2, *ws, own, got, block, partner,
        flops=8 * HROWS * HD, name=f"back{bit}",
    )


def total_kernel(*refs):
    result = refs[0][...]
    for ref in refs[1:-1]:
        result = result + ref[...]
    refs[-1][...] = result


def total(arrays, name):
    return call(total_kernel, sds(arrays[0].shape), *arrays, flops=arrays[0].size, name=name)


def local_kernel(
    q_ref, k_ref, v_ref, dsum_ref, gate_ref, pair_ref, open_ref, s0, a1, a2, a3, a4, o1, o2, o3, o4,
    gq_ref, gk_ref, gv_ref
):
    usable = usable_rows(flag_rows(s0, (a1, a2, a3, a4)))

    def step(n, h, own):
        q, k, v = q_ref[:, cut(h)], k_ref[:, cut(h)], v_ref[:, cut(h)]
        cols = head_columns(gate_ref, h)
        mask = pair_ref[...]
        raw, left, g0, first = local_weights(q, k, cols, mask)
        wh, wl = split(by_columns(raw, left, g0))
        dh, dm, dl = split3(dsum_ref[:, cut(h)])
        dots = dot(lanes(dh, dm, dl), lanes(v, v, v), NT)
        bh, bl = split(by_columns(dots * mask, left, g0))
        grad_q = dot(bh, k) + dot(bl, k)
        gk_ref[:, cut(h)] = dot(bh, q, TN) + dot(bl, q, TN)
        both = dot(wh, lanes(dh, dm), TN)
        gv_ref[:, cut(h)] = both[:, :HD] + both[:, HD:] + dot(wl, dh, TN)

        open_mask = open_ref[...]
        refs = (a1, a2, a3, a4) if own else (o1, o2, o3, o4)
        states = [s0[cut(h), :]] + [r[cut(n), :] for r in refs]
        sh, sl = split(rows(*states))
        back_all = dot(lanes(dh, dh, dm), lanes(sh, sl, sh), NT)
        for b in range(BITS):
            part = back_all[:, b * HD : (b + 1) * HD]
            grad_q = grad_q + level_weight(cols, open_mask, usable[b], b) * part
        gq_ref[:, cut(h)] = grad_q.astype(BF16)

    per_head(step)


def local_grads(q, k, v, dsum, gate, pair, is_open, first, own, other):
    return call(
        local_kernel, [sds((ROWS, FROWS), BF16), sds((ROWS, FROWS)), sds((ROWS, FROWS))],
        q, k, v, dsum, gate, pair, is_open, first, *own, *other, flops=60 * ROWS * HD * FROWS,
        name="local_grads",
    )


def final_kernel(own_ref, other_ref, o_ref):
    start = core() * HROWS
    o_ref[pl.ds(pl.multiple_of(start, HROWS), HROWS), :] = own_ref[:HROWS, :] * SCALE
    o_ref[pl.ds(pl.multiple_of(HROWS - start, HROWS), HROWS), :] = other_ref[:HROWS, :] * SCALE


def final(own, other):
    return call(final_kernel, sds((FROWS, HD)), own, other, flops=FROWS * HD, name="final")


def ends_kernel(k_ref, v_ref, gk_ref, gv_ref, keys_ref, wa, wo, d0, s0, ok_ref, ov_ref):
    lower = core() == 0
    flag = s0[FROWS : FROWS + 1, :]
    keep = jnp.where(lower, 1.0 - flag, jnp.ones_like(flag))
    mask = keys_ref[...]

    def step(n, h, own):
        grad = (wa if own else wo)[cut(n), :] * keep + d0[cut(h), :]
        high, low = split(grad)
        k, v = k_ref[:, cut(h)], v_ref[:, cut(h)]
        by_value = dot(lanes(v, v), lanes(high, low), NT)
        by_key = dot(lanes(k, k), rows(high, low))
        ok_ref[:, cut(h)] = (gk_ref[:, cut(h)] + mask * by_value).astype(BF16)
        ov_ref[:, cut(h)] = (gv_ref[:, cut(h)] + mask * by_key).astype(BF16)

    per_head(step)


def ends(k, v, gk, gv, keys, w_own, w_other, d0, first):
    return call(
        ends_kernel, [sds((ROWS, FROWS), BF16)] * 2, k, v, gk, gv, keys, w_own, w_other, d0, first,
        flops=8 * ROWS * HD * FROWS, name="ends",
    )


def project_kernel(x_ref, d_ref, own_ref, other_ref):
    high, low = split(d_ref[...])
    stacked = rows(high, low)
    first = core() == 0

    def chip(p, carry):
        x = x_ref[:, cut(p)]
        grad = dot(rows(x, x), stacked, TN)
        upper, lower = grad[:SHARE], grad[SHARE:]
        at = pl.ds(pl.multiple_of(p * SHARE, SHARE), SHARE)
        own_ref[at, :] = jnp.where(first, upper, lower)
        other_ref[at, :] = jnp.where(first, lower, upper)
        return carry

    lax.fori_loop(0, 16, chip, 0, unroll=2)


def project(x, dlog):
    return call(
        project_kernel, [sds((16 * SHARE, HD))] * 2, x, dlog, flops=4 * x.size * HD, name="project"
    )


def halve_kernel(side_of, length):
    def kernel(a_ref, b_ref, keep_ref, send_ref):
        side = side_of()
        keep = pl.ds(pl.multiple_of(side * length, length), length)
        send = pl.ds(pl.multiple_of((1 - side) * length, length), length)
        keep_ref[...] = a_ref[keep, :] + b_ref[keep, :]
        send_ref[...] = a_ref[send, :] + b_ref[send, :]

    return kernel


def halve(a, b, bit):
    length = a.shape[0] // 2
    return call(
        halve_kernel(lambda: bit_of(bit), length), [sds((length, HD))] * 2, a, b, flops=a.size,
        name=f"halve{bit}",
    )


def widen_kernel(a_ref, b_ref, o_ref):
    o_ref[:, :HD] = a_ref[...] + b_ref[...]
    o_ref[:, HD:] = jnp.zeros((SHARE, LEVELS * HEADS - HD), F32)


def widen(a, b):
    return call(widen_kernel, sds((SHARE, LEVELS * HEADS)), a, b, flops=1000, name="widen")


FLIP = (0b1, 0b10, 0b110, 0b1000, 0b11000)


def swap(value, bit, name):
    with jax.named_scope(name):
        return lax.ppermute(value, "seq", [(i, i ^ FLIP[bit]) for i in range(32)])


def swap_y(value, flip, name):
    with jax.named_scope(name):
        return lax.ppermute(value, "dp", [(i, i ^ flip) for i in range(4)])


def hold(value, *others):
    return lax.optimization_barrier((value, *others))[0]


def body(queries, key_vectors, value_vectors, features, w_level, offsets, cotangent, final_grad):
    q, k, v, g = (a.reshape(ROWS, FROWS) for a in (queries, key_vectors, value_vectors, cotangent))
    x = features.reshape(ROWS, -1)
    fg = final_grad.reshape(FROWS, HD)

    mine, keys, is_open, pair = tails(offsets, k, v)
    first = swap(mine, 0, "turn0")
    blocks = {1: join(mine, first, 0)}
    own, other = [], []
    for b in range(1, BITS):
        got = swap(blocks[b], b, f"up{b}")
        if b == 1:
            gate, slope = gates(x, w_level.T)
            got = hold(got, gate)
        elif b == 2:
            same, near = intra(q, k, v, pair)
            got = hold(got, same)
        elif b == 4:
            mix, *prods = low_levels(same, near, q, gate, is_open, first, own[:3], other[:3])
            got = hold(got, mix)
        own.append(got)
        other.append(swap(got, 0, f"turn{b}"))
        if b < BITS - 1:
            blocks[b + 1] = join(blocks[b], got, b)

    normed, dsum, prod4, da4, do4 = top_level(mix, q, g, gate, is_open, first, own, other[3])
    d_own, d_other = [None, None, None, da4], [None, None, None, do4]
    ws = [fg]
    for b in reversed(range(1, BITS)):
        got = swap(d_other[b - 1], 0, f"half{b}")
        to_partner, kept = back(b, ws, d_own[b - 1], got, blocks[b], own[b - 1])
        moved = swap(to_partner, b, f"down{b}")
        if b == 4:
            dlog = gate_grads(dsum, same, near, [*prods, prod4], slope, is_open, first, own)
            share, send = project(x, dlog)
            send = swap(send, 0, "share")
            d0, *rest = state_grads(q, hold(dsum, share), gate, is_open, first, own[:3])
            d_own[:3], d_other[:3] = rest[:3], rest[3:]
            moved = hold(moved, d0)
        elif b == 3:
            share, send = halve(share, send, 4)
            send = swap(send, 4, "share4")
            grad_q, gk, gv = local_grads(
                q, k, v, hold(dsum, share), gate, pair, is_open, first, own, other
            )
            moved = hold(moved, gk)
        elif b == 2:
            blocks[5] = join(blocks[4], own[3], 4)
            fin_other = swap(blocks[5], 0, "fin")
            d0_got = lax.ppermute(d0, "seq", [(i + 1, i) for i in range(0, 32, 2)])
            share, send = halve(share, send, 3)
            send = swap(send, 3, "share3")
            share, send = halve(share, send, 2)
            moved = hold(moved, share, blocks[5])
        else:
            send = swap(send, 2, "share2")
            fin = final(blocks[5], fin_other)
            share, send = halve(share, send, 1)
            send = swap(send, 1, "share1")
            moved = hold(moved, share, fin)
        ws = [kept, moved]
    w_own = total(ws, "w_chip")
    w_other = swap(w_own, 0, "half0")

    row = total([share, send], "row")
    row = total([row, swap_y(row, 3, "share_y2")], "row2")
    grad_level = widen(row, swap_y(row, 1, "share_y1"))

    grad_k, grad_v = ends(k, v, gk, gv, keys, w_own, w_other, d0_got, first)
    flat = (1, ROWS, FROWS)
    return (
        normed.reshape(flat),
        grad_q.reshape(flat),
        grad_k.reshape(flat),
        grad_v.reshape(flat),
        grad_level,
        fin.reshape(1, HEADS, HD, HD),
    )


def solution(mesh):
    wide = P("dp", "seq", None)
    state = P("dp", None, None, None)
    return jax.shard_map(
        body,
        mesh=mesh,
        in_specs=(wide, wide, wide, wide, P(), P("dp", "seq"), wide, state),
        out_specs=(wide, wide, wide, wide, P("seq", None), state),
        check_vma=False,
    )
```

```python
import functools

import jax
import jax.numpy as jnp
from jax import lax
from jax.experimental import pallas as pl
from jax.experimental.pallas import tpu as pltpu
from jax.sharding import PartitionSpec as P

HEADS = 12
HALF = HEADS // 2
HD = 128
STRETCH = 128
ROWS = 2 * STRETCH
LEVELS = 12
BITS = 5
HROWS = HALF * HD
FROWS = HEADS * HD
SHARE = 64
EPS = 1e-06
SCALE = 0.0625
F32 = jnp.float32
BF16 = jnp.bfloat16

NN = (((1,), (0,)), ((), ()))
NT = (((1,), (1,)), ((), ()))
TN = (((0,), (0,)), ((), ()))


def dot(a, b, dims=NN):
    return lax.dot_general(a, b, dims, preferred_element_type=F32)


def split(a):
    high = a.astype(BF16)
    return high, (a - high.astype(F32)).astype(BF16)


def split3(a):
    high = a.astype(BF16)
    rest = a - high.astype(F32)
    middle = rest.astype(BF16)
    return high, middle, (rest - middle.astype(F32)).astype(BF16)


def lanes(*parts):
    return jnp.concatenate(parts, axis=1)


def rows(*parts):
    return jnp.concatenate(parts, axis=0)


def seq_index():
    return lax.axis_index("seq").astype(jnp.int32)


def bit_of(b):
    return lax.rem(lax.shift_right_logical(seq_index(), b), 2)


def core():
    return bit_of(0)


def chip_x():
    return lax.rem(lax.shift_right_logical(seq_index(), 1), 4)


def chip_z():
    return lax.shift_right_logical(seq_index(), 3)


def sds(shape, dtype=F32):
    return jax.ShapeDtypeStruct(shape, dtype)


def call(kernel, out_shape, *args, scratch=(), flops=0, name=None, smem=()):
    outs = out_shape if isinstance(out_shape, (list, tuple)) else [out_shape]
    size = sum(a.size * a.dtype.itemsize for a in args)
    size += sum(s.size * jnp.dtype(s.dtype).itemsize for s in outs)
    in_specs = [
        pl.BlockSpec(memory_space=pltpu.SMEM if n in smem else pltpu.VMEM) for n in range(len(args))
    ]
    out_specs = [pl.BlockSpec(memory_space=pltpu.VMEM) for _ in outs]
    with jax.named_scope(name):
        return pl.pallas_call(
            kernel,
            in_specs=in_specs,
            out_specs=out_specs if isinstance(out_shape, (list, tuple)) else out_specs[0],
            scratch_shapes=list(scratch),
            out_shape=out_shape,
            compiler_params=pltpu.CompilerParams(vmem_limit_bytes=16 * 2**20),
            cost_estimate=pl.CostEstimate(flops=flops, bytes_accessed=size, transcendentals=0),
            name=name,
        )(*args)


def per_head(step, unroll=2, own=True, other=True):
    half = core() * HALF

    def own_half(n, carry):
        step(n, half + n, True)
        return carry

    def other_half(n, carry):
        step(n, HALF - half + n, False)
        return carry

    if own:
        lax.fori_loop(0, HALF, own_half, 0, unroll=unroll)
    if other:
        lax.fori_loop(0, HALF, other_half, 0, unroll=unroll)


def cut(n):
    return pl.ds(pl.multiple_of(n * HD, HD), HD)


def tails_kernel(off_ref, k_ref, v_ref, o_ref, keys_ref, open_ref, pair_ref):
    off0, off1 = off_ref[0, 0], off_ref[0, 1]
    t = lax.broadcasted_iota(jnp.int32, (ROWS, HD), 0)
    second = t >= STRETCH
    u = jnp.where(second, t - STRETCH, t)
    off = jnp.where(second, off1, off0)
    inside = jnp.where(off < STRETCH, jnp.where(u >= off, 1.0, 0.0), 0.0)
    kept = jnp.where(off < STRETCH, inside, 1.0)
    f0, f1 = (off0 < STRETCH).astype(F32), (off1 < STRETCH).astype(F32)
    keys = kept * jnp.where(second, 1.0, 1.0 - f1)
    keys_ref[...] = keys
    open_ref[...] = (1.0 - inside) * jnp.where(second, 1.0 - f0, 1.0)

    def head(h, carry):
        kept_keys = (k_ref[:, cut(h)].astype(F32) * keys).astype(BF16)
        o_ref[cut(h), :] = dot(kept_keys, v_ref[:, cut(h)], TN)
        return carry

    lax.fori_loop(0, HEADS, head, 0, unroll=3)
    o_ref[FROWS : FROWS + 8, :] = jnp.full((8, HD), jnp.maximum(f0, f1), F32)

    t = lax.broadcasted_iota(jnp.int32, (ROWS, ROWS), 0)
    s = lax.broadcasted_iota(jnp.int32, (ROWS, ROWS), 1)
    t2, s2 = t >= STRETCH, s >= STRETCH
    ut, us = jnp.where(t2, t - STRETCH, t), jnp.where(s2, s - STRETCH, s)
    t_off, s_off = jnp.where(t2, off1, off0), jnp.where(s2, off1, off0)
    t_in = jnp.where(t_off < STRETCH, jnp.where(ut >= t_off, 1, 0), 0)
    s_in = jnp.where(s_off < STRETCH, jnp.where(us >= s_off, 1, 0), 0)
    s_kept = jnp.where(s_off < STRETCH, s_in, 1)
    same = jnp.where(ut >= us, 1, 0) * (1 - t_in * (1 - s_in))
    cross = (1 - t_in) * s_kept * jnp.where(t2, 1, 0)
    both = jnp.where(t2, 1, 0) == jnp.where(s2, 1, 0)
    pair_ref[...] = jnp.where(both, same, cross).astype(F32)


def tails(offsets, k, v):
    return call(
        tails_kernel,
        [sds((FROWS + 8, HD)), sds((ROWS, HD)), sds((ROWS, HD)), sds((ROWS, ROWS))],
        offsets, k, v, flops=2 * ROWS * HD * FROWS, name="tails", smem=(0,),
    )


def joined(own, other, own_flag, other_flag, upper):
    own_by = jnp.where(upper, jnp.ones_like(other_flag), 1.0 - other_flag)
    other_by = jnp.where(upper, 1.0 - own_flag, jnp.ones_like(own_flag))
    return own * own_by + other * other_by


def join_first_kernel(a_ref, b_ref, o_ref):
    upper = core() == 1
    half = pl.ds(pl.multiple_of(core() * HROWS, HROWS), HROWS)
    af, bf = a_ref[FROWS:, :], b_ref[FROWS:, :]
    o_ref[:HROWS, :] = joined(a_ref[half, :], b_ref[half, :], af[0:1], bf[0:1], upper)
    o_ref[HROWS:, :] = jnp.maximum(af, bf)


def join_kernel(bit):
    def kernel(a_ref, b_ref, o_ref):
        upper = bit_of(bit) == 1
        af, bf = a_ref[HROWS:, :], b_ref[HROWS:, :]
        o_ref[:HROWS, :] = joined(a_ref[:HROWS, :], b_ref[:HROWS, :], af[0:1], bf[0:1], upper)
        o_ref[HROWS:, :] = jnp.maximum(af, bf)

    return kernel


def join(own, other, bit):
    kernel = join_kernel(bit) if bit else join_first_kernel
    return call(kernel, sds((HROWS + 8, HD)), own, other, flops=4 * HROWS * HD, name=f"join{bit}")


def gates_kernel(x_ref, w_ref, gate_ref, slope_ref):
    logit = dot(x_ref[...], w_ref[:HD, :], NT)
    gate_ref[...] = jax.nn.softplus(logit)
    slope_ref[...] = 1.0 / (1.0 + jnp.exp(-logit))


def gates(x, w):
    return call(
        gates_kernel, [sds((ROWS, HD))] * 2, x, w, flops=2 * x.size * HD, name="gates"
    )


def head_columns(gate_ref, h):
    return pltpu.roll(gate_ref[...], lax.rem(HD - h, HD), axis=1)


def column(rolled, slot):
    return rolled[:, slot * HEADS : slot * HEADS + 1]


def local_weights(q, k, gate_cols, mask):
    first = lax.broadcasted_iota(jnp.int32, (ROWS, 1), 0) < STRETCH
    g0, g1 = column(gate_cols, 0), column(gate_cols, 1)
    left = jnp.where(first, g0, g1)
    raw = dot(q, k, NT) * mask
    return raw, left, g0, first


def by_columns(a, left, right):
    return lanes(a[:, :HD] * left, a[:, HD:] * right)


def intra_kernel(q_ref, k_ref, v_ref, pair_ref, same_ref, near_ref):
    low, high = slice(0, STRETCH), slice(STRETCH, ROWS)

    def head(h, carry):
        raw = dot(q_ref[:, cut(h)], k_ref[:, cut(h)], NT) * pair_ref[...]
        v0, v1 = v_ref[low, cut(h)], v_ref[high, cut(h)]
        for out, a, v in (
            (same_ref.at[low, cut(h)], raw[low, :HD], v0),
            (same_ref.at[high, cut(h)], raw[high, HD:], v1),
            (near_ref.at[:, cut(h)], raw[high, :HD], v0),
        ):
            out[...] = dot(lanes(*split3(a)), rows(v, v, v))
        return carry

    lax.fori_loop(0, HEADS, head, 0, unroll=2)


def intra(q, k, v, pair):
    return call(
        intra_kernel, [sds((ROWS, FROWS)), sds((STRETCH, FROWS))], q, k, v, pair,
        flops=6 * ROWS * ROWS * FROWS, name="intra",
    )


def usable_rows(flags):
    prefix = jnp.zeros((1, HD), F32)
    result = []
    for b, flag in enumerate(flags):
        upper = bit_of(b).astype(F32)
        result.append(upper * (1.0 - prefix))
        prefix = jnp.maximum(prefix, upper * flag)
    return result


def flag_rows(first_ref, own_refs):
    return [first_ref[FROWS : FROWS + 1, :]] + [r[HROWS : HROWS + 1, :] for r in own_refs]


def level_weight(cols, mask, usable, b):
    return column(cols, 2 + b) * (mask * usable)


def state_products(q, states):
    high, middle, low = zip(*[split3(s) for s in states])
    return dot(lanes(q, q, q), rows(lanes(*high), lanes(*middle), lanes(*low)))


def low_levels_kernel(
    same_ref, near_ref, q_ref, gate_ref, open_ref, s0, a1, a2, a3, o1, o2, o3, mix_ref, p0, p1, p2, p3
):
    usable = usable_rows(flag_rows(s0, (a1, a2, a3)))
    mask = open_ref[...]

    def step(n, h, own):
        cols = head_columns(gate_ref, h)
        refs = (a1, a2, a3) if own else (o1, o2, o3)
        states = [s0[cut(h), :]] + [r[cut(n), :] for r in refs]
        prod = state_products(q_ref[:, cut(h)], states)
        near = column(cols, 1)[STRETCH:] * near_ref[:, cut(h)]
        mixed = column(cols, 0) * same_ref[:, cut(h)] + rows(jnp.zeros((STRETCH, HD), F32), near)
        for b, ref in enumerate((p0, p1, p2, p3)):
            part = prod[:, b * HD : (b + 1) * HD]
            ref[:, cut(h)] = part
            mixed = mixed + level_weight(cols, mask, usable[b], b) * part
        mix_ref[:, cut(h)] = mixed

    per_head(step)


def low_levels(same, near, q, gate, is_open, first, own, other):
    return call(
        low_levels_kernel, [sds((ROWS, FROWS))] * 5, same, near, q, gate, is_open, first, *own,
        *other, flops=16 * ROWS * HD * FROWS, name="low_levels",
    )


def top_level_kernel(own_half, *refs):
    mix_ref, q_ref, g_ref, gate_ref, open_ref, s0, a1, a2, a3, a4, state = refs[:11]
    norm_ref, dsum_ref, p4, grad_ref = refs[-4:]
    usable = usable_rows(flag_rows(s0, (a1, a2, a3, a4)))
    mask = open_ref[...]

    def step(n, h, own):
        cols = head_columns(gate_ref, h)
        weight = level_weight(cols, mask, usable[4], 4)
        q = q_ref[:, cut(h)]
        prod = state_products(q, [state[cut(n), :]])
        p4[:, cut(n)] = prod
        mixed = mix_ref[:, cut(h)] + weight * prod
        scale = lax.rsqrt(jnp.mean(mixed * mixed, axis=1, keepdims=True) + EPS)
        normed = mixed * scale
        norm_ref[:, cut(n if own_half else h)] = normed.astype(BF16)
        g = g_ref[:, cut(h)].astype(F32)
        dsum = scale * (g - normed * jnp.mean(g * normed, axis=1, keepdims=True))
        dsum_ref[:, cut(n)] = dsum
        high, low = split(weight * dsum)
        grad_ref[cut(n), :] = dot(rows(q, q), rows(high, low), TN)
        if not own_half:
            norm_ref[:, cut(HALF * core() + n)] = refs[11][:, cut(n)]

    per_head(step, own=own_half, other=not own_half)


def top_level(mix, q, g, gate, is_open, first, own, state, own_norm=None):
    wide = sds((ROWS, HROWS))
    args = [mix, q, g, gate, is_open, first, *own, state]
    if own_norm is not None:
        args.append(own_norm)
    return call(
        functools.partial(top_level_kernel, own_norm is None),
        [sds((ROWS, HROWS if own_norm is None else FROWS), BF16), wide, wide, sds((HROWS, HD))],
        *args, flops=4 * ROWS * HD * FROWS,
        name="top_own" if own_norm is None else "top_other",
    )


def gate_grads_kernel(
    dsum_own, dsum_other, same_ref, near_ref, p0, p1, p2, p3, p4_own, p4_other, slope_ref,
    open_ref, s0, a1, a2, a3, a4, out
):
    usable = usable_rows(flag_rows(s0, (a1, a2, a3, a4)))
    lane = lax.broadcasted_iota(jnp.int32, (ROWS, HD), 1)
    out[...] = jnp.zeros((ROWS, HD), F32)

    def step(n, h, own):
        dsum = (dsum_own if own else dsum_other)[:, cut(n)]
        near = jnp.sum(dsum[STRETCH:] * near_ref[:, cut(h)], axis=1, keepdims=True)
        values = [
            jnp.sum(dsum * same_ref[:, cut(h)], axis=1, keepdims=True),
            rows(jnp.zeros((STRETCH, 1), F32), near),
        ]
        for ref in (p0, p1, p2, p3):
            values.append(jnp.sum(dsum * ref[:, cut(h)], axis=1, keepdims=True))
        top = (p4_own if own else p4_other)[:, cut(n)]
        values.append(jnp.sum(dsum * top, axis=1, keepdims=True))
        spread = out[...]
        for slot, value in enumerate(values):
            spread = jnp.where(lane == slot * HEADS + h, value, spread)
        out[...] = spread

    per_head(step)
    factor = slope_ref[...]
    mask = open_ref[...]
    for b in range(BITS):
        start = (2 + b) * HEADS
        at_level = jnp.where(lane >= start, jnp.where(lane < start + HEADS, 1.0, 0.0), 0.0)
        factor = factor * (1.0 - at_level + at_level * (mask * usable[b]))
    out[...] = out[...] * factor


def gate_grads(dsums, same, near, prods, slope, is_open, first, own):
    return call(
        gate_grads_kernel, sds((ROWS, HD)), *dsums, same, near, *prods, slope, is_open, first,
        *own, flops=14 * ROWS * FROWS, name="gate_grads",
    )


def state_grads_kernel(
    q_ref, dsum_own, dsum_other, gate_ref, open_ref, s0, a1, a2, a3, d0, da1, da2, da3, do1, do2,
    do3
):
    usable = usable_rows(flag_rows(s0, (a1, a2, a3)))
    mask = open_ref[...]

    def step(n, h, own):
        cols = head_columns(gate_ref, h)
        dsum = (dsum_own if own else dsum_other)[:, cut(n)]
        parts = [level_weight(cols, mask, usable[b], b) * dsum for b in range(4)]
        high, low = split(lanes(*parts))
        q = q_ref[:, cut(h)]
        grad = dot(rows(q, q), rows(high, low), TN)
        d0[cut(h), :] = grad[:, :HD]
        for m, ref in enumerate((da1, da2, da3) if own else (do1, do2, do3)):
            ref[cut(n), :] = grad[:, (m + 1) * HD : (m + 2) * HD]

    per_head(step)


def state_grads(q, dsums, gate, is_open, first, own):
    half = sds((HROWS, HD))
    return call(
        state_grads_kernel, [sds((FROWS, HD))] + [half] * 6, q, *dsums, gate, is_open, first, *own,
        flops=16 * ROWS * HD * FROWS, name="state_grads",
    )


def back_kernel(bit):
    def kernel(*refs):
        if bit == BITS - 1:
            fg_ref, own_ref, got_ref, b_ref, p_ref, to_ref, keep_ref = refs
            on_first = (lax.shift_right_logical(seq_index(), 1) == 0).astype(F32)
            half = pl.ds(pl.multiple_of(core() * HROWS, HROWS), HROWS)
            w = fg_ref[half, :].astype(F32) * (SCALE * on_first)
        else:
            w1_ref, w2_ref, own_ref, got_ref, b_ref, p_ref, to_ref, keep_ref = refs
            w = w1_ref[...] + w2_ref[...]
        upper = bit_of(bit) == 1
        own_keep = 1.0 - b_ref[HROWS : HROWS + 1, :]
        partner_keep = 1.0 - p_ref[HROWS : HROWS + 1, :]
        one = jnp.ones_like(own_keep)
        grad = (own_ref[...] + got_ref[...]) * upper.astype(F32)
        to_ref[...] = w * jnp.where(upper, own_keep, one) + grad
        keep_ref[...] = w * jnp.where(upper, one, partner_keep)

    return kernel


def back(bit, ws, own, got, block, partner):
    return call(
        back_kernel(bit), [sds((HROWS, HD))] * 2, *ws, own, got, block, partner,
        flops=8 * HROWS * HD, name=f"back{bit}",
    )


def total_kernel(*refs):
    result = refs[0][...]
    for ref in refs[1:-1]:
        result = result + ref[...]
    refs[-1][...] = result


def total(arrays, name):
    return call(total_kernel, sds(arrays[0].shape), *arrays, flops=arrays[0].size, name=name)


def local_kernel(own_half, *refs):
    q_ref, k_ref, v_ref, dsum_ref, gate_ref, pair_ref, open_ref, s0 = refs[:8]
    flags, levels = refs[8:12], refs[8:12] if own_half else refs[12:16]
    gq_ref, gk_ref, gv_ref = refs[-3:]
    own_grad = None if own_half else refs[16]
    usable = usable_rows(flag_rows(s0, flags))

    def step(n, h, own):
        q, k, v = q_ref[:, cut(h)], k_ref[:, cut(h)], v_ref[:, cut(h)]
        cols = head_columns(gate_ref, h)
        mask = pair_ref[...]
        raw, left, g0, first = local_weights(q, k, cols, mask)
        wh, wl = split(by_columns(raw, left, g0))
        dh, dm, dl = split3(dsum_ref[:, cut(n)])
        dots = dot(lanes(dh, dm, dl), lanes(v, v, v), NT)
        bh, bl = split(by_columns(dots * mask, left, g0))
        grad_q = dot(bh, k) + dot(bl, k)
        gk_ref[:, cut(n)] = dot(bh, q, TN) + dot(bl, q, TN)
        both = dot(wh, lanes(dh, dm), TN)
        gv_ref[:, cut(n)] = both[:, :HD] + both[:, HD:] + dot(wl, dh, TN)

        open_mask = open_ref[...]
        states = [s0[cut(h), :]] + [r[cut(n), :] for r in levels]
        sh, sl = split(rows(*states))
        back_all = dot(lanes(dh, dh, dm), lanes(sh, sl, sh), NT)
        for b in range(BITS):
            part = back_all[:, b * HD : (b + 1) * HD]
            grad_q = grad_q + level_weight(cols, open_mask, usable[b], b) * part
        gq_ref[:, cut(n if own_half else h)] = grad_q.astype(BF16)
        if not own_half:
            gq_ref[:, cut(HALF * core() + n)] = own_grad[:, cut(n)]

    per_head(step, own=own_half, other=not own_half)


def local_grads(q, k, v, dsum, gate, pair, is_open, first, own, other=(), own_grad=None):
    args = [q, k, v, dsum, gate, pair, is_open, first, *own, *other]
    if other:
        args.append(own_grad)
    half = sds((ROWS, HROWS))
    return call(
        functools.partial(local_kernel, not other),
        [sds((ROWS, FROWS if other else HROWS), BF16), half, half], *args,
        flops=30 * ROWS * HD * FROWS, name="local_other" if other else "local_own",
    )


def final_kernel(own_ref, other_ref, o_ref):
    start = core() * HROWS
    o_ref[pl.ds(pl.multiple_of(start, HROWS), HROWS), :] = own_ref[:HROWS, :] * SCALE
    o_ref[pl.ds(pl.multiple_of(HROWS - start, HROWS), HROWS), :] = other_ref[:HROWS, :] * SCALE


def final(own, other):
    return call(final_kernel, sds((FROWS, HD)), own, other, flops=FROWS * HD, name="final")


def ends_kernel(k_ref, v_ref, gk_own, gv_own, gk_other, gv_other, keys_ref, wa, wo, d0, s0, ok_ref, ov_ref):
    lower = core() == 0
    flag = s0[FROWS : FROWS + 1, :]
    keep = jnp.where(lower, 1.0 - flag, jnp.ones_like(flag))
    mask = keys_ref[...]

    def step(n, h, own):
        grad = (wa if own else wo)[cut(n), :] * keep + d0[cut(h), :]
        high, low = split(grad)
        k, v = k_ref[:, cut(h)], v_ref[:, cut(h)]
        by_value = dot(lanes(v, v), lanes(high, low), NT)
        by_key = dot(lanes(k, k), rows(high, low))
        gk_ref, gv_ref = (gk_own, gv_own) if own else (gk_other, gv_other)
        ok_ref[:, cut(h)] = (gk_ref[:, cut(n)] + mask * by_value).astype(BF16)
        ov_ref[:, cut(h)] = (gv_ref[:, cut(n)] + mask * by_key).astype(BF16)

    per_head(step)


def ends(k, v, own, other, keys, w_own, w_other, d0, first):
    return call(
        ends_kernel, [sds((ROWS, FROWS), BF16)] * 2, k, v, *own, *other, keys, w_own,
        w_other, d0, first, flops=8 * ROWS * HD * FROWS, name="ends",
    )


def project_kernel(x_ref, d_ref, own_ref, other_ref):
    high, low = split(d_ref[...])
    stacked = rows(high, low)
    first = core() == 0

    def chip(p, carry):
        x = x_ref[:, cut(p)]
        grad = dot(rows(x, x), stacked, TN)
        upper, lower = grad[:SHARE], grad[SHARE:]
        chip_in_row = lax.rem(p, 4)
        turned = jnp.where(chip_in_row == 0, 0, lax.rem(chip_in_row, 3) + 1)
        at = pl.ds(pl.multiple_of((p - chip_in_row + turned) * SHARE, SHARE), SHARE)
        own_ref[at, :] = jnp.where(first, upper, lower)
        other_ref[at, :] = jnp.where(first, lower, upper)
        return carry

    lax.fori_loop(0, 16, chip, 0, unroll=2)


def project(x, dlog):
    return call(
        project_kernel, [sds((16 * SHARE, HD))] * 2, x, dlog, flops=4 * x.size * HD, name="project"
    )


def halve_kernel(side_of, length):
    def kernel(a_ref, b_ref, keep_ref, send_ref):
        side = side_of()
        keep = pl.ds(pl.multiple_of(side * length, length), length)
        send = pl.ds(pl.multiple_of((1 - side) * length, length), length)
        keep_ref[...] = a_ref[keep, :] + b_ref[keep, :]
        send_ref[...] = a_ref[send, :] + b_ref[send, :]

    return kernel


def outer_x():
    return lax.rem(bit_of(1) + bit_of(2), 2)


def halve(a, b, side_of, name):
    length = a.shape[0] // 2
    return call(
        halve_kernel(side_of, length), [sds((length, HD))] * 2, a, b, flops=a.size, name=name
    )


def widen_kernel(a_ref, b_ref, o_ref):
    o_ref[:, :HD] = a_ref[...] + b_ref[...]
    o_ref[:, HD:] = jnp.zeros((SHARE, LEVELS * HEADS - HD), F32)


def widen(a, b):
    return call(widen_kernel, sds((SHARE, LEVELS * HEADS)), a, b, flops=1000, name="widen")


FLIP = (0b1, 0b10, 0b110, 0b1000, 0b11000)


def swap(value, bit, name):
    with jax.named_scope(name):
        return lax.ppermute(value, "seq", [(i, i ^ FLIP[bit]) for i in range(32)])


def swap_y(value, flip, name):
    with jax.named_scope(name):
        return lax.ppermute(value, "dp", [(i, i ^ flip) for i in range(4)])


def hold(value, *others):
    return lax.optimization_barrier((value, *others))[0]


def body(queries, key_vectors, value_vectors, features, w_level, offsets, cotangent, final_grad):
    q, k, v, g = (a.reshape(ROWS, FROWS) for a in (queries, key_vectors, value_vectors, cotangent))
    x = features.reshape(ROWS, -1)
    fg = final_grad.reshape(FROWS, HD)

    mine, keys, is_open, pair = tails(offsets, k, v)
    first = swap(mine, 0, "turn0")
    blocks = {1: join(mine, first, 0)}
    own, other = [], []
    for b in range(1, BITS):
        got = swap(blocks[b], b, f"up{b}")
        if b == 1:
            gate, slope = gates(x, w_level.T)
            got = hold(got, gate)
        elif b == 2:
            same, near = intra(q, k, v, pair)
            got = hold(got, same)
        elif b == 4:
            mix, *prods = low_levels(same, near, q, gate, is_open, first, own[:3], other[:3])
            got = hold(got, mix)
        own.append(got)
        other.append(swap(got, 0, f"turn{b}"))
        if b < BITS - 1:
            blocks[b + 1] = join(blocks[b], got, b)

    own_norm, dsum_own, prod_own, da4 = top_level(mix, q, g, gate, is_open, first, own, own[3])
    normed, dsum_other, prod_other, do4 = top_level(
        mix, q, g, gate, is_open, first, own, other[3], own_norm
    )
    d_own, d_other = [None, None, None, da4], [None, None, None, do4]
    ws = [fg]
    for b in reversed(range(1, BITS)):
        got = swap(d_other[b - 1], 0, f"half{b}")
        to_partner, kept = back(b, ws, d_own[b - 1], got, blocks[b], own[b - 1])
        moved = swap(to_partner, b, f"down{b}")
        if b == 4:
            d0, *rest = state_grads(
                q, (hold(dsum_own, kept), dsum_other), gate, is_open, first, own[:3]
            )
            d_own[:3], d_other[:3] = rest[:3], rest[3:]
            dlog = gate_grads(
                (hold(dsum_own, d0), dsum_other), same, near, [*prods, prod_own, prod_other],
                slope, is_open, first, own,
            )
            share, send = project(x, dlog)
            send = swap(send, 0, "share")
            moved = hold(moved, share)
        elif b == 3:
            share, send = halve(share, send, lambda: bit_of(4), "halve_z2")
            send = swap(send, 4, "share_z2")
            part = local_grads(q, k, v, hold(dsum_own, share), gate, pair, is_open, first, own)
            blocks[5] = join(hold(blocks[4], part[1]), own[3], 4)
            fin_other = swap(blocks[5], 0, "fin")
            d0_got = lax.ppermute(d0, "seq", [(i + 1, i) for i in range(0, 32, 2)])
            share, send = halve(
                share, hold(send, blocks[5]), lambda: bit_of(3), "halve_z1"
            )
            send = swap(send, 3, "share_z1")
            moved = hold(moved, share)
        elif b == 2:
            share, send = halve(share, send, outer_x, "halve_x1")
            send = swap(send, 1, "share_x1")
            rest_part = local_grads(
                q, k, v, hold(dsum_other, share), gate, pair, is_open, first, own, other, part[0]
            )
            grad_q = rest_part[0]
            row = total([share, hold(send, grad_q)], "row")
            moved = hold(moved, row)
        else:
            row = total([row, swap_y(row, 3, "share_y2")], "row2")
            fin = final(blocks[5], hold(fin_other, row))
            share, send = halve(
                row, hold(swap_y(row, 1, "share_y1"), fin), lambda: bit_of(2), "halve_x2"
            )
            send = swap(send, 2, "share_x2")
            moved = hold(moved, share)
        ws = [kept, moved]
    w_own = total(ws, "w_chip")
    w_other = swap(w_own, 0, "half0")
    grad_level = widen(share, send)

    grad_k, grad_v = ends(k, v, part[1:], rest_part[1:], keys, w_own, w_other, d0_got, first)
    flat = (1, ROWS, FROWS)
    return (
        normed.reshape(flat),
        grad_q.reshape(flat),
        grad_k.reshape(flat),
        grad_v.reshape(flat),
        grad_level,
        fin.reshape(1, HEADS, HD, HD),
    )


def solution(mesh):
    wide = P("dp", "seq", None)
    state = P("dp", None, None, None)
    return jax.shard_map(
        body,
        mesh=mesh,
        in_specs=(wide, wide, wide, wide, P(), P("dp", "seq"), wide, state),
        out_specs=(wide, wide, wide, wide, P("seq", None), state),
        check_vma=False,
    )
```

```python
import functools

import jax
import jax.numpy as jnp
from jax import lax
from jax.experimental import pallas as pl
from jax.experimental.pallas import tpu as pltpu
from jax.sharding import PartitionSpec as P

HEADS = 12
HALF = HEADS // 2
HD = 128
STRETCH = 128
ROWS = 2 * STRETCH
LEVELS = 12
BITS = 5
HROWS = HALF * HD
FROWS = HEADS * HD
SHARE = 64
EPS = 1e-06
SCALE = 0.0625
F32 = jnp.float32
BF16 = jnp.bfloat16

NN = (((1,), (0,)), ((), ()))
NT = (((1,), (1,)), ((), ()))
TN = (((0,), (0,)), ((), ()))


def dot(a, b, dims=NN):
    return lax.dot_general(a, b, dims, preferred_element_type=F32)


def split(a):
    high = a.astype(BF16)
    return high, (a - high.astype(F32)).astype(BF16)


def split3(a):
    high = a.astype(BF16)
    rest = a - high.astype(F32)
    middle = rest.astype(BF16)
    return high, middle, (rest - middle.astype(F32)).astype(BF16)


def lanes(*parts):
    return jnp.concatenate(parts, axis=1)


def rows(*parts):
    return jnp.concatenate(parts, axis=0)


def seq_index():
    return lax.axis_index("seq").astype(jnp.int32)


def bit_of(b):
    return lax.rem(lax.shift_right_logical(seq_index(), b), 2)


def core():
    return bit_of(0)


def sds(shape, dtype=F32):
    return jax.ShapeDtypeStruct(shape, dtype)


def call(kernel, out_shape, *args, scratch=(), flops=0, smem=()):
    outs = out_shape if isinstance(out_shape, (list, tuple)) else [out_shape]
    size = sum(a.size * a.dtype.itemsize for a in args)
    size += sum(s.size * jnp.dtype(s.dtype).itemsize for s in outs)
    in_specs = [
        pl.BlockSpec(memory_space=pltpu.SMEM if n in smem else pltpu.VMEM) for n in range(len(args))
    ]
    out_specs = [pl.BlockSpec(memory_space=pltpu.VMEM) for _ in outs]
    return pl.pallas_call(
        kernel,
        in_specs=in_specs,
        out_specs=out_specs if isinstance(out_shape, (list, tuple)) else out_specs[0],
        scratch_shapes=list(scratch),
        out_shape=out_shape,
        compiler_params=pltpu.CompilerParams(vmem_limit_bytes=16 * 2**20),
        cost_estimate=pl.CostEstimate(flops=flops, bytes_accessed=size, transcendentals=0),
    )(*args)


def per_head(step, unroll=2, own=True, other=True):
    half = core() * HALF

    def own_half(n, carry):
        step(n, half + n, True)
        return carry

    def other_half(n, carry):
        step(n, HALF - half + n, False)
        return carry

    if own:
        lax.fori_loop(0, HALF, own_half, 0, unroll=unroll)
    if other:
        lax.fori_loop(0, HALF, other_half, 0, unroll=unroll)


def cut(n):
    return pl.ds(pl.multiple_of(n * HD, HD), HD)


def tails_kernel(off_ref, k_ref, v_ref, o_ref, keys_ref, open_ref, pair_ref):
    off0, off1 = off_ref[0, 0], off_ref[0, 1]
    t = lax.broadcasted_iota(jnp.int32, (ROWS, HD), 0)
    second = t >= STRETCH
    u = jnp.where(second, t - STRETCH, t)
    off = jnp.where(second, off1, off0)
    inside = jnp.where(off < STRETCH, jnp.where(u >= off, 1.0, 0.0), 0.0)
    kept = jnp.where(off < STRETCH, inside, 1.0)
    f0, f1 = (off0 < STRETCH).astype(F32), (off1 < STRETCH).astype(F32)
    keys = kept * jnp.where(second, 1.0, 1.0 - f1)
    keys_ref[...] = keys
    open_ref[...] = (1.0 - inside) * jnp.where(second, 1.0 - f0, 1.0)

    def head(h, carry):
        kept_keys = (k_ref[:, cut(h)].astype(F32) * keys).astype(BF16)
        o_ref[cut(h), :] = dot(kept_keys, v_ref[:, cut(h)], TN)
        return carry

    lax.fori_loop(0, HEADS, head, 0, unroll=3)
    o_ref[FROWS : FROWS + 8, :] = jnp.full((8, HD), jnp.maximum(f0, f1), F32)

    t = lax.broadcasted_iota(jnp.int32, (ROWS, ROWS), 0)
    s = lax.broadcasted_iota(jnp.int32, (ROWS, ROWS), 1)
    t2, s2 = t >= STRETCH, s >= STRETCH
    ut, us = jnp.where(t2, t - STRETCH, t), jnp.where(s2, s - STRETCH, s)
    t_off, s_off = jnp.where(t2, off1, off0), jnp.where(s2, off1, off0)
    t_in = jnp.where(t_off < STRETCH, jnp.where(ut >= t_off, 1, 0), 0)
    s_in = jnp.where(s_off < STRETCH, jnp.where(us >= s_off, 1, 0), 0)
    s_kept = jnp.where(s_off < STRETCH, s_in, 1)
    same = jnp.where(ut >= us, 1, 0) * (1 - t_in * (1 - s_in))
    cross = (1 - t_in) * s_kept * jnp.where(t2, 1, 0)
    both = jnp.where(t2, 1, 0) == jnp.where(s2, 1, 0)
    pair_ref[...] = jnp.where(both, same, cross).astype(F32)


def tails(offsets, k, v):
    return call(
        tails_kernel,
        [sds((FROWS + 8, HD)), sds((ROWS, HD)), sds((ROWS, HD)), sds((ROWS, ROWS))],
        offsets, k, v, flops=2 * ROWS * HD * FROWS, smem=(0,),
    )


def joined(own, other, own_flag, other_flag, upper):
    own_by = jnp.where(upper, jnp.ones_like(other_flag), 1.0 - other_flag)
    other_by = jnp.where(upper, 1.0 - own_flag, jnp.ones_like(own_flag))
    return own * own_by + other * other_by


def join_first_kernel(a_ref, b_ref, o_ref):
    upper = core() == 1
    half = pl.ds(pl.multiple_of(core() * HROWS, HROWS), HROWS)
    af, bf = a_ref[FROWS:, :], b_ref[FROWS:, :]
    o_ref[:HROWS, :] = joined(a_ref[half, :], b_ref[half, :], af[0:1], bf[0:1], upper)
    o_ref[HROWS:, :] = jnp.maximum(af, bf)


def join_kernel(bit):
    def kernel(a_ref, b_ref, o_ref):
        upper = bit_of(bit) == 1
        af, bf = a_ref[HROWS:, :], b_ref[HROWS:, :]
        o_ref[:HROWS, :] = joined(a_ref[:HROWS, :], b_ref[:HROWS, :], af[0:1], bf[0:1], upper)
        o_ref[HROWS:, :] = jnp.maximum(af, bf)

    return kernel


def join(own, other, bit):
    kernel = join_kernel(bit) if bit else join_first_kernel
    return call(kernel, sds((HROWS + 8, HD)), own, other, flops=4 * HROWS * HD)


def gates_kernel(x_ref, w_ref, gate_ref, slope_ref):
    logit = dot(x_ref[...], w_ref[:HD, :], NT)
    gate_ref[...] = jax.nn.softplus(logit)
    slope_ref[...] = 1.0 / (1.0 + jnp.exp(-logit))


def gates(x, w):
    return call(gates_kernel, [sds((ROWS, HD))] * 2, x, w, flops=2 * x.size * HD)


def head_columns(gate_ref, h):
    return pltpu.roll(gate_ref[...], lax.rem(HD - h, HD), axis=1)


def column(rolled, slot):
    return rolled[:, slot * HEADS : slot * HEADS + 1]


def local_weights(q, k, gate_cols, mask):
    first = lax.broadcasted_iota(jnp.int32, (ROWS, 1), 0) < STRETCH
    g0, g1 = column(gate_cols, 0), column(gate_cols, 1)
    left = jnp.where(first, g0, g1)
    raw = dot(q, k, NT) * mask
    return raw, left, g0, first


def by_columns(a, left, right):
    return lanes(a[:, :HD] * left, a[:, HD:] * right)


def intra_kernel(q_ref, k_ref, v_ref, pair_ref, same_ref, near_ref):
    low, high = slice(0, STRETCH), slice(STRETCH, ROWS)

    def head(h, carry):
        raw = dot(q_ref[:, cut(h)], k_ref[:, cut(h)], NT) * pair_ref[...]
        v0, v1 = v_ref[low, cut(h)], v_ref[high, cut(h)]
        for out, a, v in (
            (same_ref.at[low, cut(h)], raw[low, :HD], v0),
            (same_ref.at[high, cut(h)], raw[high, HD:], v1),
            (near_ref.at[:, cut(h)], raw[high, :HD], v0),
        ):
            out[...] = dot(lanes(*split3(a)), rows(v, v, v))
        return carry

    lax.fori_loop(0, HEADS, head, 0, unroll=2)


def intra(q, k, v, pair):
    return call(
        intra_kernel, [sds((ROWS, FROWS)), sds((STRETCH, FROWS))], q, k, v, pair,
        flops=6 * ROWS * ROWS * FROWS,
    )


def usable_rows(flags):
    prefix = jnp.zeros((1, HD), F32)
    result = []
    for b, flag in enumerate(flags):
        upper = bit_of(b).astype(F32)
        result.append(upper * (1.0 - prefix))
        prefix = jnp.maximum(prefix, upper * flag)
    return result


def flag_rows(first_ref, own_refs):
    return [first_ref[FROWS : FROWS + 1, :]] + [r[HROWS : HROWS + 1, :] for r in own_refs]


def level_weight(cols, mask, usable, b):
    return column(cols, 2 + b) * (mask * usable)


def state_products(q, states):
    high, middle, low = zip(*[split3(s) for s in states])
    return dot(lanes(q, q, q), rows(lanes(*high), lanes(*middle), lanes(*low)))


def low_levels_kernel(
    same_ref, near_ref, q_ref, gate_ref, open_ref, s0, a1, a2, a3, o1, o2, o3, mix_ref, p0, p1, p2, p3
):
    usable = usable_rows(flag_rows(s0, (a1, a2, a3)))
    mask = open_ref[...]

    def step(n, h, own):
        cols = head_columns(gate_ref, h)
        refs = (a1, a2, a3) if own else (o1, o2, o3)
        states = [s0[cut(h), :]] + [r[cut(n), :] for r in refs]
        prod = state_products(q_ref[:, cut(h)], states)
        near = column(cols, 1)[STRETCH:] * near_ref[:, cut(h)]
        mixed = column(cols, 0) * same_ref[:, cut(h)] + rows(jnp.zeros((STRETCH, HD), F32), near)
        for b, ref in enumerate((p0, p1, p2, p3)):
            part = prod[:, b * HD : (b + 1) * HD]
            ref[:, cut(h)] = part
            mixed = mixed + level_weight(cols, mask, usable[b], b) * part
        mix_ref[:, cut(h)] = mixed

    per_head(step)


def low_levels(same, near, q, gate, is_open, first, own, other):
    return call(
        low_levels_kernel, [sds((ROWS, FROWS))] * 5, same, near, q, gate, is_open, first, *own,
        *other, flops=16 * ROWS * HD * FROWS,
    )


def top_level_kernel(own_half, *refs):
    mix_ref, q_ref, g_ref, gate_ref, open_ref, s0, a1, a2, a3, a4, state = refs[:11]
    norm_ref, dsum_ref, p4, grad_ref = refs[-4:]
    usable = usable_rows(flag_rows(s0, (a1, a2, a3, a4)))
    mask = open_ref[...]

    def step(n, h, own):
        cols = head_columns(gate_ref, h)
        weight = level_weight(cols, mask, usable[4], 4)
        q = q_ref[:, cut(h)]
        prod = state_products(q, [state[cut(n), :]])
        p4[:, cut(n)] = prod
        mixed = mix_ref[:, cut(h)] + weight * prod
        scale = lax.rsqrt(jnp.mean(mixed * mixed, axis=1, keepdims=True) + EPS)
        normed = mixed * scale
        norm_ref[:, cut(n if own_half else h)] = normed.astype(BF16)
        g = g_ref[:, cut(h)].astype(F32)
        dsum = scale * (g - normed * jnp.mean(g * normed, axis=1, keepdims=True))
        dsum_ref[:, cut(n)] = dsum
        high, low = split(weight * dsum)
        grad_ref[cut(n), :] = dot(rows(q, q), rows(high, low), TN)
        if not own_half:
            norm_ref[:, cut(HALF * core() + n)] = refs[11][:, cut(n)]

    per_head(step, unroll=3, own=own_half, other=not own_half)


def top_level(mix, q, g, gate, is_open, first, own, state, own_norm=None):
    wide = sds((ROWS, HROWS))
    args = [mix, q, g, gate, is_open, first, *own, state]
    if own_norm is not None:
        args.append(own_norm)
    return call(
        functools.partial(top_level_kernel, own_norm is None),
        [sds((ROWS, HROWS if own_norm is None else FROWS), BF16), wide, wide, sds((HROWS, HD))],
        *args, flops=4 * ROWS * HD * FROWS,
    )


def gate_grads_kernel(
    dsum_own, dsum_other, same_ref, near_ref, p0, p1, p2, p3, p4_own, p4_other, slope_ref,
    open_ref, s0, a1, a2, a3, a4, out
):
    usable = usable_rows(flag_rows(s0, (a1, a2, a3, a4)))
    lane = lax.broadcasted_iota(jnp.int32, (ROWS, HD), 1)
    out[...] = jnp.zeros((ROWS, HD), F32)

    def step(n, h, own):
        dsum = (dsum_own if own else dsum_other)[:, cut(n)]
        near = jnp.sum(dsum[STRETCH:] * near_ref[:, cut(h)], axis=1, keepdims=True)
        values = [
            jnp.sum(dsum * same_ref[:, cut(h)], axis=1, keepdims=True),
            rows(jnp.zeros((STRETCH, 1), F32), near),
        ]
        for ref in (p0, p1, p2, p3):
            values.append(jnp.sum(dsum * ref[:, cut(h)], axis=1, keepdims=True))
        top = (p4_own if own else p4_other)[:, cut(n)]
        values.append(jnp.sum(dsum * top, axis=1, keepdims=True))
        spread = out[...]
        for slot, value in enumerate(values):
            spread = jnp.where(lane == slot * HEADS + h, value, spread)
        out[...] = spread

    per_head(step)
    factor = slope_ref[...]
    mask = open_ref[...]
    for b in range(BITS):
        start = (2 + b) * HEADS
        at_level = jnp.where(lane >= start, jnp.where(lane < start + HEADS, 1.0, 0.0), 0.0)
        factor = factor * (1.0 - at_level + at_level * (mask * usable[b]))
    out[...] = out[...] * factor


def gate_grads(dsums, same, near, prods, slope, is_open, first, own):
    return call(
        gate_grads_kernel, sds((ROWS, HD)), *dsums, same, near, *prods, slope, is_open, first,
        *own, flops=14 * ROWS * FROWS,
    )


def state_grads_kernel(
    q_ref, dsum_own, dsum_other, gate_ref, open_ref, s0, a1, a2, a3, d0, da1, da2, da3, do1, do2,
    do3
):
    usable = usable_rows(flag_rows(s0, (a1, a2, a3)))
    mask = open_ref[...]

    def step(n, h, own):
        cols = head_columns(gate_ref, h)
        dsum = (dsum_own if own else dsum_other)[:, cut(n)]
        parts = [level_weight(cols, mask, usable[b], b) * dsum for b in range(4)]
        high, low = split(lanes(*parts))
        q = q_ref[:, cut(h)]
        grad = dot(rows(q, q), rows(high, low), TN)
        d0[cut(h), :] = grad[:, :HD]
        for m, ref in enumerate((da1, da2, da3) if own else (do1, do2, do3)):
            ref[cut(n), :] = grad[:, (m + 1) * HD : (m + 2) * HD]

    per_head(step)


def state_grads(q, dsums, gate, is_open, first, own):
    half = sds((HROWS, HD))
    return call(
        state_grads_kernel, [sds((FROWS, HD))] + [half] * 6, q, *dsums, gate, is_open, first, *own,
        flops=16 * ROWS * HD * FROWS,
    )


def back_kernel(bit):
    def kernel(*refs):
        if bit == BITS - 1:
            fg_ref, own_ref, got_ref, b_ref, p_ref, to_ref, keep_ref = refs
            on_first = (lax.shift_right_logical(seq_index(), 1) == 0).astype(F32)
            half = pl.ds(pl.multiple_of(core() * HROWS, HROWS), HROWS)
            w = fg_ref[half, :].astype(F32) * (SCALE * on_first)
        else:
            w1_ref, w2_ref, own_ref, got_ref, b_ref, p_ref, to_ref, keep_ref = refs
            w = w1_ref[...] + w2_ref[...]
        upper = bit_of(bit) == 1
        own_keep = 1.0 - b_ref[HROWS : HROWS + 1, :]
        partner_keep = 1.0 - p_ref[HROWS : HROWS + 1, :]
        one = jnp.ones_like(own_keep)
        grad = (own_ref[...] + got_ref[...]) * upper.astype(F32)
        to_ref[...] = w * jnp.where(upper, own_keep, one) + grad
        keep_ref[...] = w * jnp.where(upper, one, partner_keep)

    return kernel


def back(bit, ws, own, got, block, partner):
    return call(
        back_kernel(bit), [sds((HROWS, HD))] * 2, *ws, own, got, block, partner,
        flops=8 * HROWS * HD,
    )


def total_kernel(*refs):
    result = refs[0][...]
    for ref in refs[1:-1]:
        result = result + ref[...]
    refs[-1][...] = result


def total(arrays):
    return call(total_kernel, sds(arrays[0].shape), *arrays, flops=arrays[0].size)


def local_kernel(own_half, *refs):
    q_ref, k_ref, v_ref, dsum_ref, gate_ref, pair_ref, open_ref, s0 = refs[:8]
    flags, levels = refs[8:12], refs[8:12] if own_half else refs[12:16]
    gq_ref, gk_ref, gv_ref = refs[-3:]
    own_grad = None if own_half else refs[16]
    usable = usable_rows(flag_rows(s0, flags))

    def step(n, h, own):
        q, k, v = q_ref[:, cut(h)], k_ref[:, cut(h)], v_ref[:, cut(h)]
        cols = head_columns(gate_ref, h)
        mask = pair_ref[...]
        raw, left, g0, _ = local_weights(q, k, cols, mask)
        wh, wl = split(by_columns(raw, left, g0))
        dh, dm, dl = split3(dsum_ref[:, cut(n)])
        dots = dot(lanes(dh, dm, dl), lanes(v, v, v), NT)
        bh, bl = split(by_columns(dots * mask, left, g0))
        grad_q = dot(bh, k) + dot(bl, k)
        gk_ref[:, cut(n)] = dot(bh, q, TN) + dot(bl, q, TN)
        both = dot(wh, lanes(dh, dm), TN)
        gv_ref[:, cut(n)] = both[:, :HD] + both[:, HD:] + dot(wl, dh, TN)

        open_mask = open_ref[...]
        states = [s0[cut(h), :]] + [r[cut(n), :] for r in levels]
        sh, sl = split(rows(*states))
        back_all = dot(lanes(dh, dh, dm), lanes(sh, sl, sh), NT)
        for b in range(BITS):
            part = back_all[:, b * HD : (b + 1) * HD]
            grad_q = grad_q + level_weight(cols, open_mask, usable[b], b) * part
        gq_ref[:, cut(n if own_half else h)] = grad_q.astype(BF16)
        if not own_half:
            gq_ref[:, cut(HALF * core() + n)] = own_grad[:, cut(n)]

    per_head(step, own=own_half, other=not own_half)


def local_grads(q, k, v, dsum, gate, pair, is_open, first, own, other=(), own_grad=None):
    args = [q, k, v, dsum, gate, pair, is_open, first, *own, *other]
    if other:
        args.append(own_grad)
    half = sds((ROWS, HROWS))
    return call(
        functools.partial(local_kernel, not other),
        [sds((ROWS, FROWS if other else HROWS), BF16), half, half], *args,
        flops=30 * ROWS * HD * FROWS,
    )


def final_kernel(own_ref, other_ref, o_ref):
    start = core() * HROWS
    o_ref[pl.ds(pl.multiple_of(start, HROWS), HROWS), :] = own_ref[:HROWS, :] * SCALE
    o_ref[pl.ds(pl.multiple_of(HROWS - start, HROWS), HROWS), :] = other_ref[:HROWS, :] * SCALE


def final(own, other):
    return call(final_kernel, sds((FROWS, HD)), own, other, flops=FROWS * HD)


def ends_kernel(k_ref, v_ref, gk_own, gv_own, gk_other, gv_other, keys_ref, wa, wo, d0, s0, ok_ref, ov_ref):
    lower = core() == 0
    flag = s0[FROWS : FROWS + 1, :]
    keep = jnp.where(lower, 1.0 - flag, jnp.ones_like(flag))
    mask = keys_ref[...]

    def step(n, h, own):
        grad = (wa if own else wo)[cut(n), :] * keep + d0[cut(h), :]
        high, low = split(grad)
        k, v = k_ref[:, cut(h)], v_ref[:, cut(h)]
        by_value = dot(lanes(v, v), lanes(high, low), NT)
        by_key = dot(lanes(k, k), rows(high, low))
        gk_ref, gv_ref = (gk_own, gv_own) if own else (gk_other, gv_other)
        ok_ref[:, cut(h)] = (gk_ref[:, cut(n)] + mask * by_value).astype(BF16)
        ov_ref[:, cut(h)] = (gv_ref[:, cut(n)] + mask * by_key).astype(BF16)

    per_head(step)


def ends(k, v, own, other, keys, w_own, w_other, d0, first):
    return call(
        ends_kernel, [sds((ROWS, FROWS), BF16)] * 2, k, v, *own, *other, keys, w_own,
        w_other, d0, first, flops=8 * ROWS * HD * FROWS,
    )


def project_kernel(x_ref, d_ref, own_ref, other_ref):
    high, low = split(d_ref[...])
    stacked = rows(high, low)
    first = core() == 0

    def chip(p, carry):
        x = x_ref[:, cut(p)]
        grad = dot(rows(x, x), stacked, TN)
        upper, lower = grad[:SHARE], grad[SHARE:]
        chip_in_row = lax.rem(p, 4)
        turned = jnp.where(chip_in_row == 0, 0, lax.rem(chip_in_row, 3) + 1)
        at = pl.ds(pl.multiple_of((p - chip_in_row + turned) * SHARE, SHARE), SHARE)
        own_ref[at, :] = jnp.where(first, upper, lower)
        other_ref[at, :] = jnp.where(first, lower, upper)
        return carry

    lax.fori_loop(0, 16, chip, 0, unroll=2)


def project(x, dlog):
    return call(project_kernel, [sds((16 * SHARE, HD))] * 2, x, dlog, flops=4 * x.size * HD)


def halve_kernel(side_of, length):
    def kernel(a_ref, b_ref, keep_ref, send_ref):
        side = side_of()
        keep = pl.ds(pl.multiple_of(side * length, length), length)
        send = pl.ds(pl.multiple_of((1 - side) * length, length), length)
        keep_ref[...] = a_ref[keep, :] + b_ref[keep, :]
        send_ref[...] = a_ref[send, :] + b_ref[send, :]

    return kernel


def outer_x():
    return lax.rem(bit_of(1) + bit_of(2), 2)


def halve(a, b, side_of):
    length = a.shape[0] // 2
    return call(halve_kernel(side_of, length), [sds((length, HD))] * 2, a, b, flops=a.size)


def widen_kernel(a_ref, b_ref, o_ref):
    o_ref[:, :HD] = a_ref[...] + b_ref[...]
    o_ref[:, HD:] = jnp.zeros((SHARE, LEVELS * HEADS - HD), F32)


def widen(a, b):
    return call(widen_kernel, sds((SHARE, LEVELS * HEADS)), a, b, flops=1000)


FLIP = (0b1, 0b10, 0b110, 0b1000, 0b11000)


def swap(value, bit):
    return lax.ppermute(value, "seq", [(i, i ^ FLIP[bit]) for i in range(32)])


def swap_y(value, flip):
    return lax.ppermute(value, "dp", [(i, i ^ flip) for i in range(4)])


def hold(value, *others):
    return lax.optimization_barrier((value, *others))[0]


def steps(queries, key_vectors, value_vectors, features, w_level, offsets, cotangent, final_grad):
    q, k, v, g = (a.reshape(ROWS, FROWS) for a in (queries, key_vectors, value_vectors, cotangent))
    x = features.reshape(ROWS, -1)
    fg = final_grad.reshape(FROWS, HD)

    mine, keys, is_open, pair = tails(offsets, k, v)
    first = swap(mine, 0)
    blocks = {1: join(mine, first, 0)}
    own, other = [], []
    for b in range(1, BITS):
        got = swap(blocks[b], b)
        if b == 1:
            gate, slope = gates(x, w_level.T)
            got = hold(got, gate)
        elif b == 2:
            same, near = intra(q, k, v, pair)
            got = hold(got, same)
        elif b == 4:
            mix, *prods = low_levels(same, near, q, gate, is_open, first, own[:3], other[:3])
            got = hold(got, mix)
        own.append(got)
        other.append(swap(got, 0))
        if b < BITS - 1:
            blocks[b + 1] = join(blocks[b], got, b)

    own_norm, dsum_own, prod_own, da4 = top_level(mix, q, g, gate, is_open, first, own, own[3])
    normed, dsum_other, prod_other, do4 = top_level(
        mix, q, g, gate, is_open, first, own, other[3], own_norm
    )
    d_own, d_other = [None, None, None, da4], [None, None, None, do4]
    ws = [fg]
    for b in reversed(range(1, BITS)):
        got = swap(d_other[b - 1], 0)
        to_partner, kept = back(b, ws, d_own[b - 1], got, blocks[b], own[b - 1])
        moved = swap(to_partner, b)
        if b == 4:
            d0, *rest = state_grads(
                q, (hold(dsum_own, kept), dsum_other), gate, is_open, first, own[:3]
            )
            d_own[:3], d_other[:3] = rest[:3], rest[3:]
            dlog = gate_grads(
                (hold(dsum_own, d0), dsum_other), same, near, [*prods, prod_own, prod_other],
                slope, is_open, first, own,
            )
            share, send = project(x, dlog)
            send = swap(send, 0)
            moved = hold(moved, share)
        elif b == 3:
            share, send = halve(share, send, lambda: bit_of(4))
            send = swap(send, 4)
            part = local_grads(q, k, v, hold(dsum_own, share), gate, pair, is_open, first, own)
            rest_part = local_grads(
                q, k, v, hold(dsum_other, part[1]), gate, pair, is_open, first, own, other, part[0]
            )
            grad_q = rest_part[0]
            share, send = halve(share, hold(send, grad_q), lambda: bit_of(3))
            send = swap(send, 3)
            moved = hold(moved, grad_q)
        elif b == 2:
            share, send = halve(share, send, outer_x)
            send = swap(send, 1)
            blocks[5] = join(hold(blocks[4], share), own[3], 4)
            fin_other = swap(blocks[5], 0)
            d0_got = lax.ppermute(d0, "seq", [(i + 1, i) for i in range(0, 32, 2)])
            row = total([share, hold(send, blocks[5])])
            moved = hold(moved, row, d0_got)
        else:
            row = total([row, swap_y(row, 3)])
            fin = final(blocks[5], hold(fin_other, row))
            share, send = halve(row, hold(swap_y(row, 1), fin), lambda: bit_of(2))
            send = swap(send, 2)
            moved = hold(moved, fin)
        ws = [kept, moved]
    w_own = total(ws)
    w_other = swap(w_own, 0)
    grad_k, grad_v = ends(k, v, part[1:], rest_part[1:], keys, w_own, w_other, d0_got, first)
    grad_level = widen(share, hold(send, grad_k))
    flat = (1, ROWS, FROWS)
    return (
        normed.reshape(flat),
        grad_q.reshape(flat),
        grad_k.reshape(flat),
        grad_v.reshape(flat),
        grad_level,
        fin.reshape(1, HEADS, HD, HD),
    )


def solution(mesh):
    wide = P("dp", "seq", None)
    state = P("dp", None, None, None)
    return jax.shard_map(
        steps,
        mesh=mesh,
        in_specs=(wide, wide, wide, wide, P(), P("dp", "seq"), wide, state),
        out_specs=(wide, wide, wide, wide, P("seq", None), state),
        check_vma=False,
    )
```
